256 devices in a mesh: fsdp: 128 (over x, z, y), tp: 2 (over core).
Axes of the slice: x: 4, y: 4, z: 8, core: 2. Of those that a mesh axis runs over, the one named last changes fastest.
Arguments:
- gate_gradient: bfloat16 [48, 524288], P(None, ('fsdp', 'tp')), may hold values from -40 to 40
- gate_velocity: float32 [48, 524288], P(None, ('fsdp', 'tp')), may hold values from -6 to 6
- rate_factor_gradient: bfloat16 [96, 196608], P(None, ('fsdp', 'tp')), may hold values from -40 to 40
- rate_factor_velocity: float32 [96, 196608], P(None, ('fsdp', 'tp')), may hold values from -6 to 6
- value_gradient: bfloat16 [48, 131072], P(None, ('fsdp', 'tp')), may hold values from -40 to 40
- value_velocity: float32 [48, 131072], P(None, ('fsdp', 'tp')), may hold values from -6 to 6
- vector_weights: float32 [933888], P(('fsdp', 'tp')), may hold values from -6 to 6
- vector_gradient: bfloat16 [933888], P(('fsdp', 'tp')), may hold values from -6 to 6
- vector_first_moment: float32 [933888], P(('fsdp', 'tp')), may hold values from -4 to 4
- vector_second_moment: float32 [933888], P(('fsdp', 'tp')), may hold values from 0.05 to 2
Outputs:
- update_gate: float32 [48, 524288], P(None, ('fsdp', 'tp'))
- update_lora: float32 [96, 196608], P(None, ('fsdp', 'tp'))
- update_value: float32 [48, 131072], P(None, ('fsdp', 'tp'))
- momentum_gate_out: float32 [48, 524288], P(None, ('fsdp', 'tp'))
- momentum_lora_out: float32 [96, 196608], P(None, ('fsdp', 'tp'))
- momentum_value_out: float32 [48, 131072], P(None, ('fsdp', 'tp'))
- vec_param_out: float32 [933888], P(('fsdp', 'tp'))
- vec_first_out: float32 [933888], P(('fsdp', 'tp'))
- vec_second_out: float32 [933888], P(('fsdp', 'tp'))
The draws below stay inside these ranges and needn't reach their ends.
All inputs are finite; a program needn't handle non-finite values.
Results may differ from the reference program's by a relative error of at most 0.0032.
Values may be sent and summed in bfloat16 or wider, within the bound.
A program may use at most 64 MiB of HBM per device.

```python
import math
import jax
import jax.numpy as jnp
from jax import lax

MODEL_WIDTH = 2048
RG = 256
RATE_RANK = 96
RV = 64
NS_STEPS = 5
GATES = 48
RATE_FACTORS = 96
VALUES = 48
VECS = 456


def scaled_sample(key, matrix_count, row_total):
    row_key, col_key, base_key = jax.random.split(key, 3)
    row_scale = jnp.exp(jax.random.uniform(row_key, (matrix_count, row_total, 1), jnp.float32, math.log(0.316), math.log(3.16)))
    col_scale = jnp.exp(jax.random.uniform(col_key, (matrix_count, 1, MODEL_WIDTH), jnp.float32, math.log(0.316), math.log(3.16)))
    base_values = jnp.clip(jax.random.normal(base_key, (matrix_count, row_total, MODEL_WIDTH), jnp.float32), -4.0, 4.0)
    values = base_values * row_scale * col_scale
    return values.reshape(matrix_count, row_total * MODEL_WIDTH).astype(jnp.bfloat16)


def draw_gate_gradient(key, part):
    return scaled_sample(jax.random.fold_in(key, 11), GATES, RG)


def draw_rate_factor_gradient(key, part):
    return scaled_sample(jax.random.fold_in(key, 23), RATE_FACTORS, RATE_RANK)


def draw_value_gradient(key, part):
    return scaled_sample(jax.random.fold_in(key, 37), VALUES, RV)


def levels(own_key, dims, shards, least, top_value):
    level = 1.0
    for position, blocks in shards:
        steps = jax.random.uniform(jax.random.fold_in(jax.random.fold_in(own_key, 6), position), (blocks,), jnp.float32, least / len(shards), top_value / len(shards))
        level = level * jnp.repeat(jnp.exp(steps), dims[position] // blocks).reshape((-1,) + (1,) * (len(dims) - 1 - position))
    return level


def scatter_about(key, shape, spread, reach, pieces=(), held_as=jnp.bfloat16):
    values = spread * jax.random.normal(key, shape, jnp.float32)
    if pieces:
        values = values * levels(key, shape, pieces, -0.22, 0.18)
    return jnp.clip(values, -reach, reach).astype(held_as)


def setup_inputs(seed: int = 0) -> dict:
    splits = jax.random.split(jax.random.key(seed), 11)
    return {
        "gate_gradient": draw_gate_gradient(jax.random.fold_in(splits[10], 71), 0),
        "gate_velocity": scatter_about(splits[1], (GATES, RG * MODEL_WIDTH), 1.0, 6.0, ((1, 256),), jnp.float32),
        "rate_factor_gradient": draw_rate_factor_gradient(jax.random.fold_in(splits[10], 71), 0),
        "rate_factor_velocity": scatter_about(splits[3], (RATE_FACTORS, RATE_RANK * MODEL_WIDTH), 1.0, 6.0, ((1, 256),), jnp.float32),
        "value_gradient": draw_value_gradient(jax.random.fold_in(splits[10], 71), 0),
        "value_velocity": scatter_about(splits[5], (VALUES, RV * MODEL_WIDTH), 1.0, 6.0, ((1, 256),), jnp.float32),
        "vector_weights": scatter_about(splits[6], (VECS * MODEL_WIDTH,), 1.0, 6.0, ((0, 256),), jnp.float32),
        "vector_gradient": scatter_about(splits[7], (VECS * MODEL_WIDTH,), 1.0, 6.0, ((0, 256),)),
        "vector_first_moment": scatter_about(splits[8], (VECS * MODEL_WIDTH,), 0.5, 4.0, ((0, 256),), jnp.float32),
        "vector_second_moment": jnp.clip(jnp.exp(math.log(2.0) - 3.6888794 * jax.random.uniform(splits[9], (VECS * MODEL_WIDTH,), jnp.float32) ** levels(splits[9], (VECS * MODEL_WIDTH,), ((0, 256),), -0.2, 0.2)), 0.05, 2.0),
    }


momentum_rate = 0.95
coef_linear = 3.4445
coef_gram = -4.775
coef_square = 2.0315
bias_first = 1.0 - 0.9 ** 10
bias_second = 1.0 - 0.95 ** 10
highest = lax.Precision.HIGHEST

def orthogonalize(blended):
    widened = blended.astype(jnp.float32)
    frobenius = jnp.sqrt(jnp.sum(widened * widened))
    current = widened / (frobenius + 1e-07)
    for iteration in range(NS_STEPS):
        gram_full = jnp.dot(current, current.T, preferred_element_type=jnp.float32, precision=highest)
        squared = jnp.dot(gram_full, gram_full, preferred_element_type=jnp.float32, precision=highest)
        poly_full = coef_gram * gram_full + coef_square * squared
        applied = jnp.dot(poly_full, current, preferred_element_type=jnp.float32, precision=highest)
        current = coef_linear * current + applied
    return current * math.sqrt(MODEL_WIDTH)

def factor_family(gradient, momentum_in, row_total):
    widened = gradient.astype(jnp.float32)
    renewed = momentum_rate * momentum_in + widened
    blended = (widened + momentum_rate * renewed).astype(jnp.bfloat16)
    matrices = blended.reshape(blended.shape[0], row_total, MODEL_WIDTH)
    updates = lax.map(orthogonalize, matrices)
    return (updates.reshape(blended.shape[0], row_total * MODEL_WIDTH), renewed)

def adamw_shard(param_in, grad_in, first_in, second_in):
    widened = grad_in.astype(jnp.float32)
    first_moment_output = 0.9 * first_in + 0.1 * widened
    second_moment_output = 0.95 * second_in + 0.05 * widened * widened
    direction = first_moment_output / bias_first / (jnp.sqrt(second_moment_output / bias_second) + 1e-08)
    parameter_output = param_in - 0.05 * (direction + 0.1 * param_in)
    return (parameter_output, first_moment_output, second_moment_output)

def reference(gate_gradient, gate_velocity, rate_factor_gradient, rate_factor_velocity, value_gradient, value_velocity, vector_weights, vector_gradient, vector_first_moment, vector_second_moment):
    gate_delta, gate_refreshed = factor_family(gate_gradient, gate_velocity, RG)
    rate_factor_delta, rate_factor_refreshed = factor_family(rate_factor_gradient, rate_factor_velocity, RATE_RANK)
    value_delta, value_refreshed = factor_family(value_gradient, value_velocity, RV)
    parameter_output, first_moment_output, second_moment_output = adamw_shard(vector_weights, vector_gradient, vector_first_moment, vector_second_moment)
    return (gate_delta, rate_factor_delta, value_delta, gate_refreshed, rate_factor_refreshed, value_refreshed, parameter_output, first_moment_output, second_moment_output)
```

```python
import functools
import math

import jax
import jax.numpy as jnp
from jax import lax
from jax.experimental import pallas as pl
from jax.experimental.pallas import tpu as pltpu
from jax.sharding import PartitionSpec as P

MODEL_WIDTH = 2048
LANES = 128
DEVICES = 256
BLOCKS = 16
PER_BLOCK = 16
NS_STEPS = 5
MESH = pl.DeviceIdType.MESH

momentum_rate = 0.95
coef_linear = 3.4445
coef_gram = -4.775
coef_square = 2.0315
bias_first = 1.0 - 0.9**10
bias_second = 1.0 - 0.95**10
highest = lax.Precision.HIGHEST

GATE_SEATS = (0, 6, 12)
RATE_SEATS = (2, 4, 8, 10, 14, 15)
VALUE_SEATS = (3, 5, 9)


def blend_columns(grad_ref, velocity_ref, column):
    piece = pl.ds(column * LANES, LANES)
    widened = grad_ref[:, piece].astype(jnp.float32)
    renewed = momentum_rate * velocity_ref[:, piece] + widened
    return widened + momentum_rate * renewed


def pack_rows(grad_ref, velocity_ref, stage, packed):
    rows, chunks = packed.shape[0], packed.shape[1]
    pitch = 16 if chunks > 8 else 8
    for column in range(chunks):
        stage[pl.ds(column, rows, stride=pitch), :] = blend_columns(
            grad_ref, velocity_ref, column
        )
    staged = stage[pl.ds(0, rows * pitch), :].reshape(rows, pitch, LANES)
    packed[...] = staged[:, :chunks, :].astype(jnp.bfloat16)


def identity(rank):
    row = lax.broadcasted_iota(jnp.int32, (rank, rank), 0)
    column = lax.broadcasted_iota(jnp.int32, (rank, rank), 1)
    return (row == column).astype(jnp.float32)


def product(left, right):
    return jnp.dot(left, right, preferred_element_type=jnp.float32, precision=highest)


def orthogonal_map(raw):
    rank = raw.shape[0]
    eye = identity(rank)
    frobenius = jnp.sqrt(jnp.sum(raw * eye))
    inverse = 1.0 / (frobenius + 1e-07)
    gram = raw * (inverse * inverse)
    total = None
    for iteration in range(NS_STEPS):
        squared = product(gram, gram)
        poly = coef_linear * eye + coef_gram * gram + coef_square * squared
        total = poly if total is None else product(poly, total)
        if iteration < NS_STEPS - 1:
            gram = product(product(poly, gram), poly)
    return total * (inverse * math.sqrt(MODEL_WIDTH))


def split_terms(values):
    first = values.astype(jnp.bfloat16)
    rest = values - first.astype(jnp.float32)
    second = rest.astype(jnp.bfloat16)
    third = (rest - second.astype(jnp.float32)).astype(jnp.bfloat16)
    return first, second, third


def exchange_kernel(
    gate_grad,
    gate_velocity,
    rate_grad,
    rate_velocity,
    value_grad,
    value_velocity,
    gate_back,
    rate_back,
    value_back,
    gate_send,
    rate_send,
    value_send,
    gate_land,
    rate_land,
    value_land,
    stage,
    matrix,
    gate_result,
    rate_result,
    value_result,
    send_sem,
    land_sem,
    result_sem,
    back_sem,
):
    me = lax.axis_index("fsdp") * 2 + lax.axis_index("tp")
    block, seat = me // PER_BLOCK, me % PER_BLOCK

    barrier = pltpu.get_barrier_semaphore()

    def greet(step, carry):
        other = (me + step) % DEVICES
        pl.semaphore_signal(
            barrier, inc=1, device_id=(other // 2, other % 2), device_id_type=MESH
        )
        return carry

    lax.fori_loop(1, DEVICES, greet, 0)

    pack_rows(gate_grad, gate_velocity, stage, gate_send)
    pack_rows(rate_grad, rate_velocity, stage, rate_send)
    pack_rows(value_grad, value_velocity, stage, value_send)

    pl.semaphore_wait(barrier, DEVICES - 1)

    kinds = (
        (GATE_SEATS, gate_send, gate_land, gate_result, gate_back, 0),
        (RATE_SEATS, rate_send, rate_land, rate_result, rate_back, 1),
        (VALUE_SEATS, value_send, value_land, value_result, value_back, 2),
    )

    for seats, send, land, result, back, index in kinds:

        def hand_out(step, carry):
            target = (block + step) % BLOCKS
            for place, offset in enumerate(seats):
                number = target * len(seats) + place
                other = target * PER_BLOCK + offset

                @pl.when(other != me)
                def _():
                    pltpu.make_async_remote_copy(
                        src_ref=send.at[number],
                        dst_ref=land.at[me],
                        send_sem=send_sem.at[index],
                        recv_sem=land_sem.at[index],
                        device_id=(other // 2, other % 2),
                        device_id_type=MESH,
                    ).start()

                @pl.when(other == me)
                def _():
                    pltpu.make_async_copy(
                        send.at[number], land.at[me], land_sem.at[index]
                    ).start()

            return carry

        lax.fori_loop(0, BLOCKS, hand_out, 0)

    def hand_back(number, result, back, index):
        pltpu.make_async_copy(result.at[me], back.at[number], back_sem.at[index]).start()

        def give(step, carry):
            other = (me + step) % DEVICES
            pltpu.make_async_remote_copy(
                src_ref=result.at[other],
                dst_ref=back.at[number],
                send_sem=result_sem.at[0],
                recv_sem=back_sem.at[index],
                device_id=(other // 2, other % 2),
                device_id_type=MESH,
            ).start()
            return carry

        lax.fori_loop(1, DEVICES, give, 0)

    def await_all(ref, sem):
        pltpu.make_async_copy(ref, ref, sem).wait()

    def solve(slabs, land, result, index, number):
        await_all(land, land_sem.at[index])
        chunks = land.shape[1]
        pitch = 16 if chunks > 8 else 8
        rank = sum(count for count, _ in slabs[0])
        view = stage.reshape(stage.shape[0] // pitch, pitch, LANES)
        view[pl.ds(0, DEVICES), pl.ds(0, chunks), :] = land[...].astype(jnp.float32)
        for column, parts in enumerate(slabs):
            row = 0
            for count, (start, stride) in parts:
                matrix[pl.ds(row, count), pl.ds(column * LANES, LANES)] = stage[
                    pl.ds(start, count, stride=stride), :
                ].astype(jnp.bfloat16)
                row += count
        whole = matrix[pl.ds(0, rank), :]
        raw = lax.dot_general(
            whole, whole, (((1,), (1,)), ((), ())), preferred_element_type=jnp.float32
        )
        terms = split_terms(orthogonal_map(raw))
        width = 512
        for start in range(0, MODEL_WIDTH, width):
            piece = matrix[pl.ds(0, rank), pl.ds(start, width)]
            update = sum(
                jnp.dot(term, piece, preferred_element_type=jnp.float32) for term in terms
            )
            for inner in range(width // LANES):
                column = start // LANES + inner
                row = 0
                for count, (offset, stride) in slabs[column]:
                    stage[pl.ds(offset, count, stride=stride), :] = update[
                        row : row + count, inner * LANES : (inner + 1) * LANES
                    ]
                    row += count
        result[...] = view[pl.ds(0, DEVICES), pl.ds(0, chunks), :].astype(jnp.bfloat16)

    gate_slabs = [[(256, (column, 16))] for column in range(16)]
    rate_slabs = []
    for column in range(16):
        parts = []
        for turn in range(3):
            chunk = 16 * turn + column
            parts.append((32, (8 * (chunk // 6) + chunk % 6, 64)))
        rate_slabs.append(parts)
    value_slabs = [
        [(64, (8 * (column // 4) + column % 4, 32))] for column in range(16)
    ]

    is_gate = seat % 6 == 0
    is_value = (seat == 3) | (seat == 5) | (seat == 9)
    is_rate = (
        (seat == 2) | (seat == 4) | (seat == 8) | (seat == 10) | (seat == 14) | (seat == 15)
    )

    @pl.when(is_gate)
    def _():
        number = block * 3 + seat // 6
        solve(gate_slabs, gate_land, gate_result, 0, number)
        hand_back(number, gate_result, gate_back, 0)

    @pl.when(is_rate)
    def _():
        number = block * 6 + (seat + seat // 15 * 3 - 1) // 3
        solve(rate_slabs, rate_land, rate_result, 1, number)
        hand_back(number, rate_result, rate_back, 1)

    @pl.when(is_value)
    def _():
        number = block * 3 + (seat - 1) // 3
        solve(value_slabs, value_land, value_result, 2, number)
        hand_back(number, value_result, value_back, 2)

    def await_sent(ref, sem):
        pltpu.make_async_copy(ref, ref, sem).wait()

    for seats, send, land, result, back, index in kinds:
        await_all(back, back_sem.at[index])

    @pl.when(is_gate)
    def _():
        await_sent(gate_send.at[pl.ds(0, 47)], send_sem.at[0])
        await_sent(gate_result.at[pl.ds(0, 255)], result_sem.at[0])

    @pl.when(jnp.logical_not(is_gate))
    def _():
        await_sent(gate_send, send_sem.at[0])

    @pl.when(is_rate)
    def _():
        await_sent(rate_send.at[pl.ds(0, 95)], send_sem.at[1])
        await_sent(rate_result.at[pl.ds(0, 255)], result_sem.at[0])

    @pl.when(jnp.logical_not(is_rate))
    def _():
        await_sent(rate_send, send_sem.at[1])

    @pl.when(is_value)
    def _():
        await_sent(value_send.at[pl.ds(0, 47)], send_sem.at[2])
        await_sent(value_result.at[pl.ds(0, 255)], result_sem.at[0])

    @pl.when(jnp.logical_not(is_value))
    def _():
        await_sent(value_send, send_sem.at[2])


def unpack_rows(back, stage, out):
    rows, chunks = back.shape[0], back.shape[1]
    pitch = 16 if chunks > 8 else 8
    view = stage.reshape(stage.shape[0] // pitch, pitch, LANES)
    view[pl.ds(0, rows), pl.ds(0, chunks), :] = back[...].astype(jnp.float32)
    for column in range(chunks):
        out[:, pl.ds(column * LANES, LANES)] = stage[pl.ds(column, rows, stride=pitch), :]


def finish_kernel(
    gate_back,
    rate_back,
    value_back,
    gate_grad,
    gate_velocity,
    rate_grad,
    rate_velocity,
    value_grad,
    value_velocity,
    gate_update,
    rate_update,
    value_update,
    gate_renewed,
    rate_renewed,
    value_renewed,
    stage,
):
    for grad, velocity, renewed in (
        (gate_grad, gate_velocity, gate_renewed),
        (rate_grad, rate_velocity, rate_renewed),
        (value_grad, value_velocity, value_renewed),
    ):
        renewed[...] = momentum_rate * velocity[...] + grad[...].astype(jnp.float32)
    unpack_rows(gate_back, stage, gate_update)
    unpack_rows(rate_back, stage, rate_update)
    unpack_rows(value_back, stage, value_update)


def adamw_shard(param_in, grad_in, first_in, second_in):
    widened = grad_in.astype(jnp.float32)
    first_moment_output = 0.9 * first_in + 0.1 * widened
    second_moment_output = 0.95 * second_in + 0.05 * widened * widened
    direction = (
        first_moment_output / bias_first / (jnp.sqrt(second_moment_output / bias_second) + 1e-08)
    )
    parameter_output = param_in - 0.05 * (direction + 0.1 * param_in)
    return (parameter_output, first_moment_output, second_moment_output)


def local(
    gate_gradient,
    gate_velocity,
    rate_factor_gradient,
    rate_factor_velocity,
    value_gradient,
    value_velocity,
    vector_weights,
    vector_gradient,
    vector_first_moment,
    vector_second_moment,
):
    vmem = pl.BlockSpec(memory_space=pltpu.VMEM)
    half, full = jnp.bfloat16, jnp.float32
    packed = ((48, 16, LANES), (96, 6, LANES), (48, 4, LANES))
    landed = tuple((DEVICES,) + shape[1:] for shape in packed)
    factors = (
        gate_gradient,
        gate_velocity,
        rate_factor_gradient,
        rate_factor_velocity,
        value_gradient,
        value_velocity,
    )
    backs = pl.pallas_call(
        exchange_kernel,
        out_shape=[jax.ShapeDtypeStruct(shape, half) for shape in packed],
        in_specs=[vmem] * 6,
        out_specs=[vmem] * 3,
        scratch_shapes=[pltpu.VMEM(shape, half) for shape in packed]
        + [pltpu.VMEM(shape, half) for shape in landed]
        + [
            pltpu.VMEM((DEVICES * 16, LANES), full),
            pltpu.VMEM((256, MODEL_WIDTH), half),
        ]
        + [pltpu.VMEM(shape, half) for shape in landed]
        + [
            pltpu.SemaphoreType.DMA((3,)),
            pltpu.SemaphoreType.DMA((3,)),
            pltpu.SemaphoreType.DMA((1,)),
            pltpu.SemaphoreType.DMA((3,)),
        ],
        compiler_params=pltpu.CompilerParams(collective_id=0, has_side_effects=True),
    )(*factors)
    updates = pl.pallas_call(
        finish_kernel,
        out_shape=[
            jax.ShapeDtypeStruct(array.shape, full)
            for array in (factors[1], factors[3], factors[5]) * 2
        ],
        in_specs=[vmem] * 9,
        out_specs=[vmem] * 6,
        scratch_shapes=[pltpu.VMEM((768, LANES), full)],
    )(*backs, *factors)
    vectors = adamw_shard(
        vector_weights, vector_gradient, vector_first_moment, vector_second_moment
    )
    return (*updates, *vectors)


def solution(mesh):
    split = P(None, ("fsdp", "tp"))
    flat = P(("fsdp", "tp"))
    return jax.shard_map(
        local,
        mesh=mesh,
        in_specs=(split,) * 6 + (flat,) * 4,
        out_specs=(split,) * 6 + (flat,) * 3,
        check_vma=False,
    )
```

```python
import functools
import math

import jax
import jax.numpy as jnp
from jax import lax
from jax.experimental import pallas as pl
from jax.experimental.pallas import tpu as pltpu
from jax.sharding import PartitionSpec as P

MODEL_WIDTH = 2048
LANES = 128
DEVICES = 256
BLOCKS = 16
PER_BLOCK = 16
NS_STEPS = 5
MESH = pl.DeviceIdType.MESH

momentum_rate = 0.95
coef_linear = 3.4445
coef_gram = -4.775
coef_square = 2.0315
bias_first = 1.0 - 0.9**10
bias_second = 1.0 - 0.95**10

GATE_SEATS = (0, 6, 12)
RATE_SEATS = (2, 4, 8, 10, 14, 15)
VALUE_SEATS = (3, 5, 9)


def blend_columns(grad_ref, velocity_ref, column):
    piece = pl.ds(column * LANES, LANES)
    widened = grad_ref[:, piece].astype(jnp.float32)
    renewed = momentum_rate * velocity_ref[:, piece] + widened
    return widened + momentum_rate * renewed


def pack_rows(grad_ref, velocity_ref, stage, packed):
    rows, chunks = packed.shape[0], packed.shape[1]
    pitch = 16 if chunks > 8 else 8
    for column in range(chunks):
        stage[pl.ds(column, rows, stride=pitch), :] = blend_columns(
            grad_ref, velocity_ref, column
        )
    staged = stage[pl.ds(0, rows * pitch), :].reshape(rows, pitch, LANES)
    packed[...] = staged[:, :chunks, :].astype(jnp.bfloat16)


def identity(rank):
    row = lax.broadcasted_iota(jnp.int32, (rank, rank), 0)
    column = lax.broadcasted_iota(jnp.int32, (rank, rank), 1)
    return (row == column).astype(jnp.float32)


def split_terms(values):
    first = values.astype(jnp.bfloat16)
    second = (values - first.astype(jnp.float32)).astype(jnp.bfloat16)
    return first, second


def product(left, right):
    def multiply(x, y):
        return jnp.dot(x, y, preferred_element_type=jnp.float32)

    (high, low), (top, rest) = left, right
    return multiply(high, top) + (multiply(high, rest) + multiply(low, top))


def orthogonal_map(raw):
    rank = raw.shape[0]
    eye = identity(rank)
    frobenius = jnp.sqrt(jnp.sum(raw * eye))
    inverse = 1.0 / (frobenius + 1e-07)
    gram = raw * (inverse * inverse)
    total = None
    for iteration in range(NS_STEPS):
        gram_terms = split_terms(gram)
        squared = product(gram_terms, gram_terms)
        poly = coef_linear * eye + coef_gram * gram + coef_square * squared
        poly_terms = split_terms(poly)
        total = poly if total is None else product(poly_terms, split_terms(total))
        if iteration < NS_STEPS - 1:
            gram = product(split_terms(product(poly_terms, gram_terms)), poly_terms)
    return total * (inverse * math.sqrt(MODEL_WIDTH))


def exchange_kernel(
    gate_grad,
    gate_velocity,
    rate_grad,
    rate_velocity,
    value_grad,
    value_velocity,
    gate_back,
    rate_back,
    value_back,
    gate_send,
    rate_send,
    value_send,
    gate_land,
    rate_land,
    value_land,
    stage,
    matrix,
    gate_result,
    rate_result,
    value_result,
    send_sem,
    land_sem,
    result_sem,
    back_sem,
):
    me = lax.axis_index("fsdp") * 2 + lax.axis_index("tp")
    block, seat = me // PER_BLOCK, me % PER_BLOCK

    barrier = pltpu.get_barrier_semaphore()

    def greet(step, carry):
        other = (me + step) % DEVICES
        pl.semaphore_signal(
            barrier, inc=1, device_id=(other // 2, other % 2), device_id_type=MESH
        )
        return carry

    lax.fori_loop(1, DEVICES, greet, 0)

    pack_rows(gate_grad, gate_velocity, stage, gate_send)
    pack_rows(rate_grad, rate_velocity, stage, rate_send)
    pack_rows(value_grad, value_velocity, stage, value_send)

    pl.semaphore_wait(barrier, DEVICES - 1)

    kinds = (
        (GATE_SEATS, gate_send, gate_land, gate_result, gate_back, 0),
        (RATE_SEATS, rate_send, rate_land, rate_result, rate_back, 1),
        (VALUE_SEATS, value_send, value_land, value_result, value_back, 2),
    )

    for seats, send, land, result, back, index in kinds:

        def hand_out(step, carry):
            target = (block + step) % BLOCKS
            for place, offset in enumerate(seats):
                number = target * len(seats) + place
                other = target * PER_BLOCK + offset

                @pl.when(other != me)
                def _():
                    pltpu.make_async_remote_copy(
                        src_ref=send.at[number],
                        dst_ref=land.at[me],
                        send_sem=send_sem.at[index],
                        recv_sem=land_sem.at[index],
                        device_id=(other // 2, other % 2),
                        device_id_type=MESH,
                    ).start()

                @pl.when(other == me)
                def _():
                    pltpu.make_async_copy(
                        send.at[number], land.at[me], land_sem.at[index]
                    ).start()

            return carry

        lax.fori_loop(0, BLOCKS, hand_out, 0)

    def hand_back(number, result, back, index):
        pltpu.make_async_copy(result.at[me], back.at[number], back_sem.at[index]).start()

        def give(step, carry):
            other = (me + step) % DEVICES
            pltpu.make_async_remote_copy(
                src_ref=result.at[other],
                dst_ref=back.at[number],
                send_sem=result_sem.at[0],
                recv_sem=back_sem.at[index],
                device_id=(other // 2, other % 2),
                device_id_type=MESH,
            ).start()
            return carry

        lax.fori_loop(1, DEVICES, give, 0)

    def await_all(ref, sem):
        pltpu.make_async_copy(ref, ref, sem).wait()

    def solve(slabs, land, result, index, number):
        await_all(land, land_sem.at[index])
        chunks = land.shape[1]
        pitch = 16 if chunks > 8 else 8
        rank = sum(count for count, _ in slabs[0])
        view = stage.reshape(stage.shape[0] // pitch, pitch, LANES)
        view[pl.ds(0, DEVICES), pl.ds(0, chunks), :] = land[...].astype(jnp.float32)
        for column, parts in enumerate(slabs):
            row = 0
            for count, (start, stride) in parts:
                matrix[pl.ds(row, count), pl.ds(column * LANES, LANES)] = stage[
                    pl.ds(start, count, stride=stride), :
                ].astype(jnp.bfloat16)
                row += count
        whole = matrix[pl.ds(0, rank), :]
        raw = lax.dot_general(
            whole, whole, (((1,), (1,)), ((), ())), preferred_element_type=jnp.float32
        )
        terms = split_terms(orthogonal_map(raw))
        width = 512
        for start in range(0, MODEL_WIDTH, width):
            piece = matrix[pl.ds(0, rank), pl.ds(start, width)]
            update = sum(
                jnp.dot(term, piece, preferred_element_type=jnp.float32) for term in terms
            )
            for inner in range(width // LANES):
                column = start // LANES + inner
                row = 0
                for count, (offset, stride) in slabs[column]:
                    stage[pl.ds(offset, count, stride=stride), :] = update[
                        row : row + count, inner * LANES : (inner + 1) * LANES
                    ]
                    row += count
        result[...] = view[pl.ds(0, DEVICES), pl.ds(0, chunks), :].astype(jnp.bfloat16)

    gate_slabs = [[(256, (column, 16))] for column in range(16)]
    rate_slabs = []
    for column in range(16):
        parts = []
        for turn in range(3):
            chunk = 16 * turn + column
            parts.append((32, (8 * (chunk // 6) + chunk % 6, 64)))
        rate_slabs.append(parts)
    value_slabs = [
        [(64, (8 * (column // 4) + column % 4, 32))] for column in range(16)
    ]

    is_gate = seat % 6 == 0
    is_value = (seat == 3) | (seat == 5) | (seat == 9)
    is_rate = (
        (seat == 2) | (seat == 4) | (seat == 8) | (seat == 10) | (seat == 14) | (seat == 15)
    )

    @pl.when(is_gate)
    def _():
        number = block * 3 + seat // 6
        solve(gate_slabs, gate_land, gate_result, 0, number)
        hand_back(number, gate_result, gate_back, 0)

    @pl.when(is_rate)
    def _():
        number = block * 6 + (seat + seat // 15 * 3 - 1) // 3
        solve(rate_slabs, rate_land, rate_result, 1, number)
        hand_back(number, rate_result, rate_back, 1)

    @pl.when(is_value)
    def _():
        number = block * 3 + (seat - 1) // 3
        solve(value_slabs, value_land, value_result, 2, number)
        hand_back(number, value_result, value_back, 2)

    def await_sent(ref, sem):
        pltpu.make_async_copy(ref, ref, sem).wait()

    for seats, send, land, result, back, index in kinds:
        await_all(back, back_sem.at[index])

    @pl.when(is_gate)
    def _():
        await_sent(gate_send.at[pl.ds(0, 47)], send_sem.at[0])
        await_sent(gate_result.at[pl.ds(0, 255)], result_sem.at[0])

    @pl.when(jnp.logical_not(is_gate))
    def _():
        await_sent(gate_send, send_sem.at[0])

    @pl.when(is_rate)
    def _():
        await_sent(rate_send.at[pl.ds(0, 95)], send_sem.at[1])
        await_sent(rate_result.at[pl.ds(0, 255)], result_sem.at[0])

    @pl.when(jnp.logical_not(is_rate))
    def _():
        await_sent(rate_send, send_sem.at[1])

    @pl.when(is_value)
    def _():
        await_sent(value_send.at[pl.ds(0, 47)], send_sem.at[2])
        await_sent(value_result.at[pl.ds(0, 255)], result_sem.at[0])

    @pl.when(jnp.logical_not(is_value))
    def _():
        await_sent(value_send, send_sem.at[2])


def unpack_rows(back, stage, out):
    rows, chunks = back.shape[0], back.shape[1]
    pitch = 16 if chunks > 8 else 8
    view = stage.reshape(stage.shape[0] // pitch, pitch, LANES)
    view[pl.ds(0, rows), pl.ds(0, chunks), :] = back[...].astype(jnp.float32)
    for column in range(chunks):
        out[:, pl.ds(column * LANES, LANES)] = stage[pl.ds(column, rows, stride=pitch), :]


def finish_kernel(
    gate_back,
    rate_back,
    value_back,
    gate_grad,
    gate_velocity,
    rate_grad,
    rate_velocity,
    value_grad,
    value_velocity,
    gate_update,
    rate_update,
    value_update,
    gate_renewed,
    rate_renewed,
    value_renewed,
    stage,
):
    for grad, velocity, renewed in (
        (gate_grad, gate_velocity, gate_renewed),
        (rate_grad, rate_velocity, rate_renewed),
        (value_grad, value_velocity, value_renewed),
    ):
        renewed[...] = momentum_rate * velocity[...] + grad[...].astype(jnp.float32)
    unpack_rows(gate_back, stage, gate_update)
    unpack_rows(rate_back, stage, rate_update)
    unpack_rows(value_back, stage, value_update)


def adamw_shard(param_in, grad_in, first_in, second_in):
    widened = grad_in.astype(jnp.float32)
    first_moment_output = 0.9 * first_in + 0.1 * widened
    second_moment_output = 0.95 * second_in + 0.05 * widened * widened
    direction = (
        first_moment_output / bias_first / (jnp.sqrt(second_moment_output / bias_second) + 1e-08)
    )
    parameter_output = param_in - 0.05 * (direction + 0.1 * param_in)
    return (parameter_output, first_moment_output, second_moment_output)


def local(
    gate_gradient,
    gate_velocity,
    rate_factor_gradient,
    rate_factor_velocity,
    value_gradient,
    value_velocity,
    vector_weights,
    vector_gradient,
    vector_first_moment,
    vector_second_moment,
):
    vmem = pl.BlockSpec(memory_space=pltpu.VMEM)
    half, full = jnp.bfloat16, jnp.float32
    packed = ((48, 16, LANES), (96, 6, LANES), (48, 4, LANES))
    landed = tuple((DEVICES,) + shape[1:] for shape in packed)
    factors = (
        gate_gradient,
        gate_velocity,
        rate_factor_gradient,
        rate_factor_velocity,
        value_gradient,
        value_velocity,
    )
    backs = pl.pallas_call(
        exchange_kernel,
        out_shape=[jax.ShapeDtypeStruct(shape, half) for shape in packed],
        in_specs=[vmem] * 6,
        out_specs=[vmem] * 3,
        scratch_shapes=[pltpu.VMEM(shape, half) for shape in packed]
        + [pltpu.VMEM(shape, half) for shape in landed]
        + [
            pltpu.VMEM((DEVICES * 16, LANES), full),
            pltpu.VMEM((256, MODEL_WIDTH), half),
        ]
        + [pltpu.VMEM(shape, half) for shape in landed]
        + [
            pltpu.SemaphoreType.DMA((3,)),
            pltpu.SemaphoreType.DMA((3,)),
            pltpu.SemaphoreType.DMA((1,)),
            pltpu.SemaphoreType.DMA((3,)),
        ],
        compiler_params=pltpu.CompilerParams(collective_id=0, has_side_effects=True),
    )(*factors)
    updates = pl.pallas_call(
        finish_kernel,
        out_shape=[
            jax.ShapeDtypeStruct(array.shape, full)
            for array in (factors[1], factors[3], factors[5]) * 2
        ],
        in_specs=[vmem] * 9,
        out_specs=[vmem] * 6,
        scratch_shapes=[pltpu.VMEM((768, LANES), full)],
    )(*backs, *factors)
    vectors = adamw_shard(
        vector_weights, vector_gradient, vector_first_moment, vector_second_moment
    )
    return (*updates, *vectors)


def solution(mesh):
    split = P(None, ("fsdp", "tp"))
    flat = P(("fsdp", "tp"))
    return jax.shard_map(
        local,
        mesh=mesh,
        in_specs=(split,) * 6 + (flat,) * 4,
        out_specs=(split,) * 6 + (flat,) * 3,
        check_vma=False,
    )
```
